32 devices in a mesh: dp: 4 (over y, core), seq: 8 (over z, x).
Axes of the slice: x: 2, y: 2, z: 4, core: 2. Of those that a mesh axis runs over, the one named last changes fastest.
Arguments:
- queries: bfloat16 [32768, 1024], P(('dp', 'seq')), parts along dimension 0, may hold values from -6 to 6
- keys: bfloat16 [32768, 1024], P(('dp', 'seq')), parts along dimension 0, may hold values from -6 to 6
- values: bfloat16 [32768, 1024], P(('dp', 'seq')), parts along dimension 0, may hold values from -6 to 6
Outputs:
- attended: bfloat16 [32768, 1024], P(('dp', 'seq')), parts along dimension 0
- far_attended: bfloat16 [1024, 1024], P(('dp', 'seq')), parts along dimension 0
The draws below stay inside these ranges and needn't reach their ends.
There are 4 independent parts, one for each index of `dp`. The reference program is written for one: setup_inputs(seed, part) draws one part's arguments, and reference() takes and returns one part's arrays. A program takes and returns all parts, laid end to end along the dimension named above; each array names one. Nothing has to cross between parts.
All inputs are finite; a program needn't handle non-finite values.
Results may differ from the reference program's by a relative error of at most 0.0095.
Values may be sent and summed in bfloat16 or wider, within the bound.
A program may use at most 192 MiB of HBM per device.

```python
import jax
import jax.numpy as jnp
import numpy as np
from jax import lax

H = 16
HD = 64
TOK_DEV = 1024
MIDDLE_DILATION = 4
OUTER_DILATION = 32
MIDDLE_SEGMENT = 8192
TOKENS = 8192


def draw_queries(key, part):
    drawn = jnp.clip(jax.random.normal(jax.random.fold_in(key, 1), (TOKENS, H, HD), jnp.float32) * 1.5, -6.0, 6.0)
    return drawn.reshape(TOKENS, H * HD).astype(jnp.bfloat16)


def draw_keys(key, part):
    drawn = jnp.clip(jax.random.normal(jax.random.fold_in(key, 2), (TOKENS, H, HD), jnp.float32) * 1.5, -6.0, 6.0)
    return drawn.reshape(TOKENS, H * HD).astype(jnp.bfloat16)


def block_levels(stream_key, shape, cuts, smallest, top_value):
    factor_of, own = 1.0, jax.random.fold_in(stream_key, 6)
    for axis_at, blocks in cuts:
        steps = jnp.exp(jax.random.uniform(jax.random.fold_in(own, axis_at), (blocks,), jnp.float32, smallest / len(cuts), top_value / len(cuts)))
        factor_of = factor_of * jnp.repeat(steps, shape[axis_at] // blocks).reshape([-1 if axis == axis_at else 1 for axis in range(len(shape))])
    return factor_of


def normal_values(key, shape, deviation, most, cuts=(), dtype=jnp.bfloat16):
    values = jax.random.normal(key, shape, jnp.float32) * deviation
    if len(cuts) > 0:
        values = block_levels(key, shape, cuts, -0.22, 0.18) * values
    return jnp.clip(values, min=-most, max=most).astype(dtype)


def setup_inputs(seed: int = 0, part: int = 0) -> dict:
    streams_of = jax.random.split(jax.random.key(seed), 4)
    part_splits = jax.random.split(jax.random.fold_in(streams_of[3], part), 4)
    queries = draw_queries(jax.random.fold_in(jax.random.fold_in(streams_of[3], part), 71), part)
    keys = draw_keys(jax.random.fold_in(jax.random.fold_in(streams_of[3], part), 71), part)
    values = normal_values(part_splits[2], (TOKENS, H * HD), 1.0, 6.0, ((0, 8),))
    return {"queries": queries, "keys": keys, "values": values}


VOID_LEVEL = -1.0e30


def attend_one(query, keys, values):
    factor = query.shape[-1] ** -0.5
    scores = jnp.einsum("qd,kd->qk", query.astype(jnp.float32), keys.astype(jnp.float32)) * factor
    peak = jnp.max(scores, axis=-1, keepdims=True)
    powers = jnp.exp(scores - peak)
    total = jnp.sum(powers, axis=-1, keepdims=True)
    rounded = lax.optimization_barrier(powers.astype(jnp.bfloat16)).astype(jnp.float32)
    mixed = jnp.einsum("qk,kd->qd", rounded, values.astype(jnp.float32)) / total
    return mixed.astype(jnp.bfloat16), peak[:, 0] + jnp.log(total[:, 0])


def attend_per_head(query, keys, values):
    return lax.map(lambda triple: attend_one(triple[0], triple[1], triple[2]), (query, keys, values))


def to_heads(array):
    length = array.shape[0]
    return array.reshape(length, H, HD).transpose(1, 0, 2)


def dilate_tokens(array, rate):
    heads, length, depth = array.shape
    offsets = np.arange(heads) % rate
    return array.reshape(heads, length // rate, rate, depth)[np.arange(heads), :, offsets, :]


def spread_back(mixed, level, rate):
    heads, count, depth = mixed.shape
    chosen = np.arange(rate)[None, :] == (np.arange(heads) % rate)[:, None]
    full_out = (mixed.astype(jnp.float32)[:, :, None, :] * chosen.astype(np.float32)[:, None, :, None]).reshape(heads, count * rate, depth)
    full_level = jnp.where(chosen[:, None, :], level[:, :, None], VOID_LEVEL).reshape(heads, count * rate)
    return full_out, full_level


def combine_levels(branches):
    peak = branches[0][1]
    for entry in branches[1:]:
        peak = jnp.maximum(peak, entry[1])
    numer = jnp.zeros(branches[0][0].shape, jnp.float32)
    denom = jnp.zeros(peak.shape, jnp.float32)
    for entry in branches:
        weight = jnp.exp(entry[1] - peak)
        numer = numer + weight[..., None] * entry[0].astype(jnp.float32)
        denom = denom + weight
    return numer / denom[..., None]


def segment_tokens(query, keys, values, seg_len):
    heads, length, depth = query.shape
    count = length // seg_len

    def split(array):
        return array.reshape(heads, count, seg_len, depth).transpose(1, 0, 2, 3)

    mixed, level = lax.map(lambda triple: attend_per_head(triple[0], triple[1], triple[2]), (split(query), split(keys), split(values)))
    return mixed.transpose(1, 0, 2, 3).reshape(heads, length, depth), level.transpose(1, 0, 2).reshape(heads, length)


def reference(queries, keys, values):
    query_per_head = to_heads(queries)
    key_per_head = to_heads(keys)
    value_per_head = to_heads(values)
    local_output, local_level = segment_tokens(query_per_head, key_per_head, value_per_head, 2 * TOK_DEV)
    central_output, central_level = segment_tokens(dilate_tokens(query_per_head, MIDDLE_DILATION), dilate_tokens(key_per_head, MIDDLE_DILATION), dilate_tokens(value_per_head, MIDDLE_DILATION), MIDDLE_SEGMENT // MIDDLE_DILATION)
    distant_output, distant_level = attend_per_head(dilate_tokens(query_per_head, OUTER_DILATION), dilate_tokens(key_per_head, OUTER_DILATION), dilate_tokens(value_per_head, OUTER_DILATION))
    merged_output = combine_levels([(local_output, local_level), spread_back(central_output, central_level, MIDDLE_DILATION), spread_back(distant_output, distant_level, OUTER_DILATION)])
    far_rows = distant_output.transpose(1, 0, 2).reshape(TOKENS // OUTER_DILATION, H * HD)
    return merged_output.transpose(1, 0, 2).reshape(TOKENS, H * HD).astype(jnp.bfloat16), far_rows
```

```python
import functools

import jax
import jax.numpy as jnp
from jax import lax
from jax.experimental import pallas as pl
from jax.experimental.pallas import tpu as pltpu
from jax.sharding import PartitionSpec as P

H = 16
HD = 64
MID = 4
FAR = 32
GROUP = 16
LOG2E = 1.4426950408889634
NT = (((1,), (1,)), ((), ()))


def pick_rows(array, rate, want):
    rows, cols = array.shape
    head = jnp.arange(cols) % (H * HD) // HD
    keep = jnp.arange(rate)[:, None] == want(head)[None, :]
    parts = array.reshape(rows // rate, rate, cols)
    return jnp.sum(jnp.where(keep[None], parts, jnp.zeros((), array.dtype)), axis=1)


def soft_step(q, k, v_ones, m, acc, factor):
    s = lax.dot_general(q, k, NT, preferred_element_type=jnp.float32)
    top = jnp.max(s, axis=1, keepdims=True)
    m_new = top if m is None else jnp.maximum(m, top)
    e = jnp.exp2((s - m_new) * factor).astype(jnp.bfloat16)
    part = jnp.dot(e, v_ones, preferred_element_type=jnp.float32)
    if m is None:
        return m_new, part
    return m_new, acc * jnp.exp2((m - m_new) * factor) + part


def attend_kernel(factor, tk, perm_ref, back_ref, q_ref, k_ref, v_ref, pk_ref, pv_ref, mk_ref, mv_ref,
                  fk_ref, fv_ref, out_ref, far_ref, qp, acc, mx, rows_out):
    pair = pl.program_id(0)
    n_rows = q_ref.shape[0]
    block = n_rows // MID
    sub = n_rows // FAR
    qp[...] = jnp.dot(perm_ref[...], q_ref[...], preferred_element_type=jnp.float32).astype(jnp.bfloat16)

    def with_ones(v):
        return jnp.concatenate([v, jnp.ones_like(v)], axis=1)

    for side in range(2):
        head = pair * 2 + side
        lane = lax.broadcasted_iota(jnp.int32, (1, 2 * HD), 1)
        mine = lane // HD == side

        def masked(q):
            return jnp.where(mine, q, jnp.zeros_like(q))

        def near(tile, _):
            rows = pl.ds(pl.multiple_of(tile * block, block), block)
            q = masked(qp[rows, :])
            m, a = None, None
            for kr, vr in ((k_ref, v_ref), (pk_ref, pv_ref)):
                for at in range(0, n_rows, tk):
                    m, a = soft_step(q, kr[at:at + tk, :], with_ones(vr[at:at + tk, :]), m, a, factor)
            acc[rows, :] = a
            mx[rows, :] = jnp.broadcast_to(m, (block, 2 * HD))
            return 0

        lax.fori_loop(0, MID, near, 0)
        base = pl.multiple_of(lax.rem(head, MID) * block, block)
        rows = pl.ds(base, block)
        q = masked(qp[rows, :])
        m, a = mx[rows, 0:1], acc[rows, :]
        for at in range(0, mk_ref.shape[0], tk):
            m, a = soft_step(q, mk_ref[at:at + tk, :], with_ones(mv_ref[at:at + tk, :]), m, a, factor)
        acc[rows, :] = a
        mx[rows, :] = jnp.broadcast_to(m, (block, 2 * HD))
        rows = pl.ds(pl.multiple_of(base + (head // MID) * sub, sub), sub)
        q = masked(qp[rows, :])
        fm, fa = soft_step(q, fk_ref[...], with_ones(fv_ref[...]), None, None, factor)
        far = (fa[:, :2 * HD] / fa[:, 2 * HD:]).astype(jnp.bfloat16)
        m, a = mx[rows, 0:1], acc[rows, :]
        top = jnp.maximum(m, fm)
        acc[rows, :] = a * jnp.exp2((m - top) * factor) + fa * jnp.exp2((fm - top) * factor)
        res = (acc[:, :2 * HD] / acc[:, 2 * HD:]).astype(jnp.bfloat16)
        if side == 0:
            far_ref[...] = far
            rows_out[...] = res
        else:
            far_ref[...] = jnp.where(mine, far, far_ref[...])
            rows_out[...] = jnp.where(mine, res, rows_out[...])
    out_ref[...] = jnp.dot(back_ref[...], rows_out[...], preferred_element_type=jnp.float32).astype(jnp.bfloat16)


def per_device(queries, keys, values):
    n = lax.axis_size("seq")
    group = min(GROUP, n)
    rows = queries.shape[0]
    swap = [(i, i ^ 1) for i in range(n)]
    pk = lax.ppermute(keys, "seq", swap)
    pv = lax.ppermute(values, "seq", swap)
    kv = jnp.concatenate([keys, values], axis=1)
    own = pick_rows(kv, MID, lambda h: h % MID)
    sets = None if group == n else [list(range(g, g + group)) for g in range(0, n, group)]
    mids = lax.all_gather(own, "seq", axis_index_groups=sets, tiled=True)
    if group == n:
        fars = pick_rows(mids, FAR // MID, lambda h: h // MID)
    else:
        fars = lax.all_gather(pick_rows(own, FAR // MID, lambda h: h // MID), "seq", tiled=True)
    spot = jnp.arange(rows)
    token = spot % (rows // FAR) * FAR + spot // (rows // FAR) % (FAR // MID) * MID + spot // (rows // MID)
    perm = (token[:, None] == spot[None, :]).astype(jnp.bfloat16)
    back = (token[None, :] == spot[:, None]).astype(jnp.bfloat16)
    wide = 2 * HD
    pairs = H // 2
    whole = lambda r: pl.BlockSpec((r, rows), lambda i: (0, 0), pipeline_mode=pl.Buffered(1))
    cols = lambda r: pl.BlockSpec((r, wide), lambda i: (0, i))
    shift = lambda r: pl.BlockSpec((r, wide), lambda i: (0, i + pairs))
    mr, fr = mids.shape[0], fars.shape[0]
    return pl.pallas_call(
        functools.partial(attend_kernel, HD ** -0.5 * LOG2E, 1024),
        grid=(pairs,),
        out_shape=(
            jax.ShapeDtypeStruct((rows, H * HD), jnp.bfloat16),
            jax.ShapeDtypeStruct((rows // FAR, H * HD), jnp.bfloat16),
        ),
        in_specs=[whole(rows), whole(rows)] + [cols(rows)] * 5 + [cols(mr), shift(mr), cols(fr), shift(fr)],
        out_specs=(cols(rows), cols(rows // FAR)),
        scratch_shapes=[
            pltpu.VMEM((rows, wide), jnp.bfloat16),
            pltpu.VMEM((rows, 2 * wide), jnp.float32),
            pltpu.VMEM((rows, wide), jnp.float32),
            pltpu.VMEM((rows, wide), jnp.bfloat16),
        ],
        compiler_params=pltpu.CompilerParams(vmem_limit_bytes=56 << 20),
    )(perm, back, queries, keys, values, pk, pv, mids, mids, fars, fars)


def solution(mesh):
    spec = P(("dp", "seq"), None)
    return jax.shard_map(per_device, mesh=mesh, in_specs=(spec, spec, spec), out_specs=(spec, spec), check_vma=False)
```

```python
import functools

import jax
import jax.numpy as jnp
from jax import lax
from jax.experimental import pallas as pl
from jax.experimental.pallas import tpu as pltpu
from jax.sharding import PartitionSpec as P

H = 16
HD = 64
MID = 4
FAR = 32
GROUP = 16
SUB = 16
TILE = SUB * FAR
BLOCK = TILE // MID
PAIRS = H // 2
WIDE = 2 * HD
CUTS = 4
PER_CUT = PAIRS // CUTS
CUT = WIDE * PER_CUT
ROWS = 256
FACTOR = HD ** -0.5 * 1.4426950408889634
NT = (((1,), (1,)), ((), ()))


def attend(q, k, v):
    s = lax.dot_general(q, k, NT, preferred_element_type=jnp.float32)
    m = jnp.max(s, axis=1, keepdims=True)
    e = jnp.exp2((s - m) * FACTOR).astype(jnp.bfloat16)
    part = jnp.dot(e, jnp.concatenate([v, jnp.ones_like(v)], axis=1), preferred_element_type=jnp.float32)
    return m, part[:, :WIDE], part[:, WIDE:]


def kernel(n, group, q_ref, k_ref, v_ref, out_ref, far_ref, pk, pv, mid, others, qp, num, den, top, perm, back,
           near_send, near_recv, mid_send, mid_recv, far_send, far_recv):
    rows = q_ref.shape[0]
    tiles = rows // TILE
    length = group // 2
    rounds = length - 2
    me = lax.axis_index("seq")
    base = me // group * group
    inside = lax.rem(me, group)
    side = lax.rem(inside, 2)
    pos = inside // 2
    partner = base + pos * 2 + 1 - side
    lane = lax.broadcasted_iota(jnp.int32, (1, WIDE), 1)
    first = lane < HD
    foreign = [lax.rem(base + group + i, n) for i in range(n - group)]

    def slot(at, u):
        return at * 2 + (side if u == 0 else 1 - side)

    def near_copy(cut, which):
        cols = pl.ds(cut * CUT, CUT)
        src, dst = ((k_ref, pk), (v_ref, pv))[which]
        return pltpu.make_async_remote_copy(
            src_ref=src.at[:, cols], dst_ref=dst.at[:, cols], send_sem=near_send.at[which, cut],
            recv_sem=near_recv.at[which, cut], device_id={"seq": partner}, device_id_type=pl.DeviceIdType.MESH)

    def line_copy(u, d, cut, right):
        at = slot(pos - d, u) if right else slot(pos + d, u)
        to = me + 2 if right else me - 2
        return pltpu.make_async_remote_copy(
            src_ref=mid.at[at, cut], dst_ref=mid.at[at, cut], send_sem=mid_send.at[int(right), u, d, cut],
            recv_sem=mid_recv.at[at, cut], device_id={"seq": to}, device_id_type=pl.DeviceIdType.MESH)

    def far_copy(i, arrived=False):
        there = foreign[i] // group * group
        at = i if arrived else lax.rem(me - there - group + 2 * n, n)
        return pltpu.make_async_remote_copy(
            src_ref=others.at[n - group], dst_ref=others.at[at], send_sem=far_send.at[i], recv_sem=far_recv.at[at],
            device_id={"seq": foreign[i]}, device_id_type=pl.DeviceIdType.MESH)

    def both(u, d, cut, act):
        @pl.when(jnp.logical_and(pos - d >= 0, pos < length - 1))
        def _():
            act(line_copy(u, d, cut, True))

        @pl.when(jnp.logical_and(pos + d < length, pos > 0))
        def _():
            act(line_copy(u, d, cut, False))

    def arrive(u, d, cut):
        @pl.when(pos - d >= 0)
        def _():
            line_copy(u, d, cut, True).wait_recv()

        @pl.when(pos + d < length)
        def _():
            line_copy(u, d, cut, False).wait_recv()

    def send(u, cut):
        both(u, 0, cut, lambda c: c.start())

    def relay(u, d, cut):
        arrive(u, d, cut)
        both(u, d, cut, lambda c: c.start())

    barrier = pltpu.get_barrier_semaphore()

    def greet(dev):
        pl.semaphore_signal(barrier, inc=1, device_id={"seq": dev}, device_id_type=pl.DeviceIdType.MESH)

    greet(partner)
    pl.when(pos > 0)(lambda: greet(me - 2))
    pl.when(pos < length - 1)(lambda: greet(me + 2))
    for dev in foreign:
        greet(dev)
    pl.semaphore_wait(barrier, 1 + len(foreign) + jnp.minimum(pos, 1) + jnp.minimum(length - 1 - pos, 1))

    for cut in range(CUTS):
        for which in range(2):
            near_copy(cut, which).start()

    def one_hot(spot, token):
        want = lax.rem(spot, SUB) * FAR + lax.rem(spot // SUB, FAR // MID) * MID + spot // BLOCK
        return jnp.where(want == token, 1.0, 0.0).astype(jnp.bfloat16)

    r = lax.broadcasted_iota(jnp.int32, (TILE, TILE), 0)
    c = lax.broadcasted_iota(jnp.int32, (TILE, TILE), 1)
    perm[...] = one_hot(r, c)
    back[...] = one_hot(c, r)

    def lanes_of(p):
        return pl.ds(pl.multiple_of(p * WIDE, WIDE), WIDE)

    def select(u, cut, keys, vals):
        def one(i, _):
            p = cut * PER_CUT + i
            at = pl.multiple_of(lax.rem(2 * p, MID) * BLOCK, 2 * BLOCK)
            pick = perm[pl.ds(at, 2 * BLOCK), :]
            for t in range(tiles):
                for which, ref in enumerate((keys, vals)):
                    got = jnp.dot(pick, ref[t * TILE:(t + 1) * TILE, lanes_of(p)], preferred_element_type=jnp.float32)
                    got = jnp.where(first, got[:BLOCK], got[BLOCK:]).astype(jnp.bfloat16)
                    mid[slot(pos, u), cut, t * BLOCK:(t + 1) * BLOCK, lanes_of(which * PER_CUT + i)] = got
            return 0

        lax.fori_loop(0, PER_CUT, one, 0)

    for cut in range(CUTS):
        select(0, cut, k_ref, v_ref)
        if cut:
            send(0, cut - 1)
    for t in range(tiles):
        span = slice(t * TILE, (t + 1) * TILE)
        for cut in range(CUTS):
            cols = slice(cut * CUT, (cut + 1) * CUT)
            qp[span, cols] = jnp.dot(perm[...], q_ref[span, cols], preferred_element_type=jnp.float32).astype(jnp.bfloat16)
    send(0, CUTS - 1)
    if n > group:
        for p in range(PAIRS):
            cut, i = divmod(p, PER_CUT)
            b = 2 * p // MID
            for t in range(tiles):
                for which in range(2):
                    cols = slice((which * PER_CUT + i) * WIDE, (which * PER_CUT + i + 1) * WIDE)
                    others[n - group, cut, t * SUB:(t + 1) * SUB, cols] = mid[
                        slot(pos, 0), cut, t * BLOCK + b * SUB:t * BLOCK + (b + 1) * SUB, cols]

    def merge(span, cols, mine, m, pn, pd):
        m0 = top[span, cols]
        t = jnp.maximum(m0, m)
        old, new = jnp.exp2((m0 - t) * FACTOR), jnp.exp2((m - t) * FACTOR)
        n1 = num[span, cols] * old + pn * new
        d1 = den[span, cols] * old + pd * new
        if mine is not None:
            t, n1, d1 = (jnp.where(mine, a, b[span, cols]) for a, b in ((t, top), (n1, num), (d1, den)))
        top[span, cols] = t
        num[span, cols] = n1
        den[span, cols] = d1

    def near(p, kr, vr, fresh):
        cols = lanes_of(p)

        def tile(i, _):
            span = pl.ds(pl.multiple_of(i * ROWS, ROWS), ROWS)
            q = qp[span, cols]
            k, v = kr[:, cols], vr[:, cols]
            ma, na, da = attend(jnp.where(first, q, jnp.zeros_like(q)), k, v)
            mb, nb, db = attend(jnp.where(first, jnp.zeros_like(q), q), k, v)
            m, pn, pd = jnp.where(first, ma, mb), jnp.where(first, na, nb), jnp.where(first, da, db)
            if fresh:
                top[span, cols] = m
                num[span, cols] = pn
                den[span, cols] = pd
            else:
                merge(span, cols, None, m, pn, pd)
            return 0

        lax.fori_loop(0, rows // ROWS, tile, 0)

    def middle(p, u):
        cols = lanes_of(p)
        cut, i = p // PER_CUT, lax.rem(p, PER_CUT)
        step = min(4, length)
        for at in range(0, length, step):
            k = jnp.concatenate([mid[slot(a, u), cut, :, lanes_of(i)] for a in range(at, at + step)], axis=0)
            v = jnp.concatenate([mid[slot(a, u), cut, :, lanes_of(i + PER_CUT)] for a in range(at, at + step)], axis=0)
            for s in range(2):
                mine = first if s == 0 else jnp.logical_not(first)
                spans = [pl.ds(pl.multiple_of(t * TILE + lax.rem(2 * p + s, MID) * BLOCK, BLOCK), BLOCK) for t in range(tiles)]
                q = jnp.concatenate([qp[x, cols] for x in spans], axis=0)
                m, pn, pd = attend(jnp.where(mine, q, jnp.zeros_like(q)), k, v)
                for t, x in enumerate(spans):
                    y = slice(t * BLOCK, (t + 1) * BLOCK)
                    merge(x, cols, mine, m[y], pn[y], pd[y])

    def far(p):
        cols = lanes_of(p)
        cut, i = p // PER_CUT, lax.rem(p, PER_CUT)
        b = 2 * p // MID

        def gather(j):
            got = [mid[a, cut, pl.ds(pl.multiple_of(t * BLOCK + b * SUB, SUB), SUB), lanes_of(j)]
                   for a in range(group) for t in range(tiles)]
            got += [others[a, cut, :, lanes_of(j)] for a in range(n - group)]
            return jnp.concatenate(got, axis=0)

        k, v = gather(i), gather(i + PER_CUT)
        kept = None
        for s in range(2):
            mine = first if s == 0 else jnp.logical_not(first)
            at = lax.rem(2 * p + s, MID) * BLOCK + b * SUB
            spans = [pl.ds(pl.multiple_of(t * TILE + at, SUB), SUB) for t in range(tiles)]
            q = jnp.concatenate([qp[x, cols] for x in spans], axis=0)
            m, pn, pd = attend(jnp.where(mine, q, jnp.zeros_like(q)), k, v)
            for t, x in enumerate(spans):
                y = slice(t * SUB, (t + 1) * SUB)
                merge(x, cols, mine, m[y], pn[y], pd[y])
            res = pn / pd
            kept = res if s == 0 else jnp.where(first, kept, res)
        far_ref[:, cols] = kept.astype(jnp.bfloat16)

    def take_near(cut):
        near_copy(cut, 0).wait_recv()
        near_copy(cut, 1).wait_recv()

    early = [(d, cut) for d in range(1, rounds + 1) for cut in range(CUTS)]
    share = -(-len(early) // PAIRS) if early else 0
    half = (rounds + 1) // 2
    low, high = range(1, half + 1), range(half + 1, rounds + 1)

    def phase_one(p, _):
        @pl.when(p == PAIRS - 3)
        def _():
            take_near(0)
            select(1, 0, pk, pv)

        near(p, k_ref, v_ref, True)
        for x in range(PAIRS):
            todo = early[x * share:(x + 1) * share]

            @pl.when(p == x)
            def _():
                for d, cut in todo:
                    relay(0, d, cut)

        @pl.when(p == PAIRS - 3)
        def _():
            send(1, 0)
        return 0

    lax.fori_loop(0, PAIRS, phase_one, 0)
    if n > group:
        for i in range(n - group):
            far_copy(i).start()
    gets = {0: 1, 3: 2, 6: 3}
    passes = {0: (low, 0), 1: (high, 0), 2: (low, 1), 3: (high, 1), 4: (low, 2), 5: (high, 2), 7: (low, 3)}

    def phase_two(p, _):
        for x, cut in gets.items():
            @pl.when(p == x)
            def _():
                take_near(cut)
                select(1, cut, pk, pv)

        for x in range(CUTS):
            @pl.when(p == x * PER_CUT)
            def _():
                if length > 1:
                    arrive(0, length - 1, x)

        near(p, pk, pv, False)
        middle(p, 0)
        for x in range(PAIRS):
            @pl.when(p == x)
            def _():
                if x in passes:
                    for d in passes[x][0]:
                        relay(1, d, passes[x][1])
                if x in gets:
                    send(1, gets[x])
        return 0

    lax.fori_loop(0, PAIRS, phase_two, 0)
    if n > group:
        for i in range(n - group):
            far_copy(i, True).wait_recv()

    def phase_three(p, _):
        for x in range(CUTS):
            @pl.when(p == x * PER_CUT)
            def _():
                if length > 1:
                    arrive(1, length - 1, x)

        middle(p, 1)
        far(p)
        cols = lanes_of(p)
        for t in range(tiles):
            span = slice(t * TILE, (t + 1) * TILE)
            res = (num[span, cols] / den[span, cols]).astype(jnp.bfloat16)
            out_ref[span, cols] = jnp.dot(back[...], res, preferred_element_type=jnp.float32).astype(jnp.bfloat16)

        @pl.when(p == 1)
        def _():
            for d in high:
                relay(1, d, CUTS - 1)
        return 0

    lax.fori_loop(0, PAIRS, phase_three, 0)
    for cut in range(CUTS):
        for which in range(2):
            near_copy(cut, which).wait_send()
        for u in range(2):
            for d in range(max(1, length - 1)):
                both(u, d, cut, lambda c: c.wait_send())
    for i in range(n - group):
        far_copy(i).wait_send()


def per_device(queries, keys, values):
    n = lax.axis_size("seq")
    group = min(GROUP, n)
    length = group // 2
    rows, cols = queries.shape
    spare = n - group
    dma = pltpu.SemaphoreType.DMA
    vmem = pl.BlockSpec(memory_space=pltpu.VMEM)
    return pl.pallas_call(
        functools.partial(kernel, n, group),
        out_shape=(
            jax.ShapeDtypeStruct((rows, cols), jnp.bfloat16),
            jax.ShapeDtypeStruct((rows // FAR, cols), jnp.bfloat16),
        ),
        in_specs=[vmem] * 3,
        out_specs=(vmem, vmem),
        scratch_shapes=[
            pltpu.VMEM((rows, cols), jnp.bfloat16),
            pltpu.VMEM((rows, cols), jnp.bfloat16),
            pltpu.VMEM((group, CUTS, rows // MID, 2 * CUT), jnp.bfloat16),
            pltpu.VMEM((spare + 1, CUTS, rows // FAR, 2 * CUT), jnp.bfloat16),
            pltpu.VMEM((rows, cols), jnp.bfloat16),
            pltpu.VMEM((rows, cols), jnp.float32),
            pltpu.VMEM((rows, cols), jnp.float32),
            pltpu.VMEM((rows, cols), jnp.float32),
            pltpu.VMEM((TILE, TILE), jnp.bfloat16),
            pltpu.VMEM((TILE, TILE), jnp.bfloat16),
            dma((2, CUTS)),
            dma((2, CUTS)),
            dma((2, 2, length, CUTS)),
            dma((group, CUTS)),
            dma((spare + 1,)),
            dma((spare + 1,)),
        ],
        compiler_params=pltpu.CompilerParams(collective_id=0, has_side_effects=True, vmem_limit_bytes=62 << 20),
    )(queries, keys, values)


def solution(mesh):
    spec = P(("dp", "seq"), None)
    return jax.shard_map(per_device, mesh=mesh, in_specs=(spec, spec, spec), out_specs=(spec, spec), check_vma=False)
```

```python
import functools

import jax
import jax.numpy as jnp
from jax import lax
from jax.experimental import pallas as pl
from jax.experimental.pallas import tpu as pltpu
from jax.sharding import PartitionSpec as P

H = 16
HD = 64
MID = 4
FAR = 32
GROUP = 16
SUB = 16
TILE = SUB * FAR
BLOCK = TILE // MID
PAIRS = H // 2
WIDE = 2 * HD
CUTS = 4
PER_CUT = PAIRS // CUTS
CUT = WIDE * PER_CUT
ROWS = 256
FACTOR = HD ** -0.5 * 1.4426950408889634
NT = (((1,), (1,)), ((), ()))


def attend(q, k, v):
    s = lax.dot_general(q, k, NT, preferred_element_type=jnp.float32)
    m = jnp.max(s, axis=1, keepdims=True)
    e = jnp.exp2((s - m) * FACTOR).astype(jnp.bfloat16)
    part = jnp.dot(e, jnp.concatenate([v, jnp.ones_like(v)], axis=1), preferred_element_type=jnp.float32)
    return m, part[:, :WIDE], part[:, WIDE:]


def kernel(n, group, q_ref, k_ref, v_ref, out_ref, far_ref, pk, pv, mid, others, qp, num, den, top, perm, back,
           near_send, near_recv, mid_send, mid_recv, far_send, far_recv, cross_send):
    rows = q_ref.shape[0]
    tiles = rows // TILE
    length = group // 2
    rounds = length - 2
    me = lax.axis_index("seq")
    base = me // group * group
    inside = lax.rem(me, group)
    side = lax.rem(inside, 2)
    pos = inside // 2
    partner = base + pos * 2 + 1 - side
    lane = lax.broadcasted_iota(jnp.int32, (1, WIDE), 1)
    first = lane < HD
    foreign = [lax.rem(base + group + i, n) for i in range(n - group)]

    def slot(at, u):
        return at * 2 + (side if u == 0 else 1 - side)

    def near_copy(cut, which):
        cols = pl.ds(cut * CUT, CUT)
        src, dst = ((k_ref, pk), (v_ref, pv))[which]
        return pltpu.make_async_remote_copy(
            src_ref=src.at[:, cols], dst_ref=dst.at[:, cols], send_sem=near_send.at[which, cut],
            recv_sem=near_recv.at[which, cut], device_id={"seq": partner}, device_id_type=pl.DeviceIdType.MESH)

    def line_copy(u, d, cut, right):
        at = slot(pos - d, u) if right else slot(pos + d, u)
        to = me + 2 if right else me - 2
        return pltpu.make_async_remote_copy(
            src_ref=mid.at[at, cut], dst_ref=mid.at[at, cut], send_sem=mid_send.at[int(right), u, d, cut],
            recv_sem=mid_recv.at[at, cut], device_id={"seq": to}, device_id_type=pl.DeviceIdType.MESH)

    def far_copy(i, arrived=False):
        there = foreign[i] // group * group
        at = i if arrived else lax.rem(me - there - group + 2 * n, n)
        return pltpu.make_async_remote_copy(
            src_ref=others.at[n - group], dst_ref=others.at[at], send_sem=far_send.at[i], recv_sem=far_recv.at[at],
            device_id={"seq": foreign[i]}, device_id_type=pl.DeviceIdType.MESH)

    def both(u, d, cut, act):
        @pl.when(jnp.logical_and(pos - d >= 0, pos < length - 1))
        def _():
            act(line_copy(u, d, cut, True))

        @pl.when(jnp.logical_and(pos + d < length, pos > 0))
        def _():
            act(line_copy(u, d, cut, False))

    def arrive(u, d, cut):
        @pl.when(pos - d >= 0)
        def _():
            line_copy(u, d, cut, True).wait_recv()

        @pl.when(pos + d < length)
        def _():
            line_copy(u, d, cut, False).wait_recv()

    def cross_copy(d, right):
        at = slot(pos - d if right else pos + d, 0)
        return pltpu.make_async_remote_copy(
            src_ref=mid.at[at, CUTS - 1], dst_ref=mid.at[at, CUTS - 1], send_sem=cross_send.at[int(right), d],
            recv_sem=mid_recv.at[at, CUTS - 1], device_id={"seq": partner}, device_id_type=pl.DeviceIdType.MESH)

    def cross(d, act):
        pl.when(pos - d >= 0)(lambda: act(cross_copy(d, True)))
        pl.when(pos + d < length)(lambda: act(cross_copy(d, False)))

    def send(u, cut):
        both(u, 0, cut, lambda c: c.start())

    def relay(u, d, cut):
        arrive(u, d, cut)
        both(u, d, cut, lambda c: c.start())
        if u == 0 and cut == CUTS - 1:
            cross(d, lambda c: c.start())

    barrier = pltpu.get_barrier_semaphore()

    def greet(dev):
        pl.semaphore_signal(barrier, inc=1, device_id={"seq": dev}, device_id_type=pl.DeviceIdType.MESH)

    greet(partner)
    pl.when(pos > 0)(lambda: greet(me - 2))
    pl.when(pos < length - 1)(lambda: greet(me + 2))
    for dev in foreign:
        greet(dev)
    pl.semaphore_wait(barrier, 1 + len(foreign) + jnp.minimum(pos, 1) + jnp.minimum(length - 1 - pos, 1))

    for cut in range(CUTS):
        for which in range(2):
            near_copy(cut, which).start()

    def one_hot(spot, token):
        want = lax.rem(spot, SUB) * FAR + lax.rem(spot // SUB, FAR // MID) * MID + spot // BLOCK
        return jnp.where(want == token, 1.0, 0.0).astype(jnp.bfloat16)

    r = lax.broadcasted_iota(jnp.int32, (TILE, TILE), 0)
    c = lax.broadcasted_iota(jnp.int32, (TILE, TILE), 1)
    perm[...] = one_hot(r, c)
    back[...] = one_hot(c, r)

    def lanes_of(p):
        return pl.ds(pl.multiple_of(p * WIDE, WIDE), WIDE)

    def select(u, cut, keys, vals):
        def one(i, _):
            p = cut * PER_CUT + i
            at = pl.multiple_of(lax.rem(2 * p, MID) * BLOCK, 2 * BLOCK)
            pick = perm[pl.ds(at, 2 * BLOCK), :]
            for t in range(tiles):
                for which, ref in enumerate((keys, vals)):
                    got = jnp.dot(pick, ref[t * TILE:(t + 1) * TILE, lanes_of(p)], preferred_element_type=jnp.float32)
                    got = jnp.where(first, got[:BLOCK], got[BLOCK:]).astype(jnp.bfloat16)
                    mid[slot(pos, u), cut, t * BLOCK:(t + 1) * BLOCK, lanes_of(which * PER_CUT + i)] = got
            return 0

        lax.fori_loop(0, PER_CUT, one, 0)

    for cut in range(CUTS):
        select(0, cut, k_ref, v_ref)
        if cut:
            send(0, cut - 1)
    for t in range(tiles):
        span = slice(t * TILE, (t + 1) * TILE)
        for cut in range(CUTS):
            cols = slice(cut * CUT, (cut + 1) * CUT)
            qp[span, cols] = jnp.dot(perm[...], q_ref[span, cols], preferred_element_type=jnp.float32).astype(jnp.bfloat16)
    send(0, CUTS - 1)
    if n > group:
        for p in range(PAIRS):
            cut, i = divmod(p, PER_CUT)
            b = 2 * p // MID
            for t in range(tiles):
                for which in range(2):
                    cols = slice((which * PER_CUT + i) * WIDE, (which * PER_CUT + i + 1) * WIDE)
                    others[n - group, cut, t * SUB:(t + 1) * SUB, cols] = mid[
                        slot(pos, 0), cut, t * BLOCK + b * SUB:t * BLOCK + (b + 1) * SUB, cols]

    def merge(span, cols, mine, m, pn, pd):
        m0 = top[span, cols]
        t = jnp.maximum(m0, m)
        old, new = jnp.exp2((m0 - t) * FACTOR), jnp.exp2((m - t) * FACTOR)
        n1 = num[span, cols] * old + pn * new
        d1 = den[span, cols] * old + pd * new
        if mine is not None:
            t, n1, d1 = (jnp.where(mine, a, b[span, cols]) for a, b in ((t, top), (n1, num), (d1, den)))
        top[span, cols] = t
        num[span, cols] = n1
        den[span, cols] = d1

    def near(p, kr, vr, fresh):
        cols = lanes_of(p)

        def tile(i, _):
            span = pl.ds(pl.multiple_of(i * ROWS, ROWS), ROWS)
            q = qp[span, cols]
            k, v = kr[:, cols], vr[:, cols]
            ma, na, da = attend(jnp.where(first, q, jnp.zeros_like(q)), k, v)
            mb, nb, db = attend(jnp.where(first, jnp.zeros_like(q), q), k, v)
            m, pn, pd = jnp.where(first, ma, mb), jnp.where(first, na, nb), jnp.where(first, da, db)
            if fresh:
                top[span, cols] = m
                num[span, cols] = pn
                den[span, cols] = pd
            else:
                merge(span, cols, None, m, pn, pd)
            return 0

        lax.fori_loop(0, rows // ROWS, tile, 0, unroll=True)

    def middle(p, u):
        cols = lanes_of(p)
        cut, i = p // PER_CUT, lax.rem(p, PER_CUT)
        step = min(4, length)
        for at in range(0, length, step):
            k = jnp.concatenate([mid[slot(a, u), cut, :, lanes_of(i)] for a in range(at, at + step)], axis=0)
            v = jnp.concatenate([mid[slot(a, u), cut, :, lanes_of(i + PER_CUT)] for a in range(at, at + step)], axis=0)
            for s in range(2):
                mine = first if s == 0 else jnp.logical_not(first)
                spans = [pl.ds(pl.multiple_of(t * TILE + lax.rem(2 * p + s, MID) * BLOCK, BLOCK), BLOCK) for t in range(tiles)]
                q = jnp.concatenate([qp[x, cols] for x in spans], axis=0)
                m, pn, pd = attend(jnp.where(mine, q, jnp.zeros_like(q)), k, v)
                for t, x in enumerate(spans):
                    y = slice(t * BLOCK, (t + 1) * BLOCK)
                    merge(x, cols, mine, m[y], pn[y], pd[y])

    def far(p):
        cols = lanes_of(p)
        cut, i = p // PER_CUT, lax.rem(p, PER_CUT)
        b = 2 * p // MID

        def gather(j):
            got = [mid[a, cut, pl.ds(pl.multiple_of(t * BLOCK + b * SUB, SUB), SUB), lanes_of(j)]
                   for a in range(group) for t in range(tiles)]
            got += [others[a, cut, :, lanes_of(j)] for a in range(n - group)]
            return jnp.concatenate(got, axis=0)

        k, v = gather(i), gather(i + PER_CUT)
        kept = None
        for s in range(2):
            mine = first if s == 0 else jnp.logical_not(first)
            at = lax.rem(2 * p + s, MID) * BLOCK + b * SUB
            spans = [pl.ds(pl.multiple_of(t * TILE + at, SUB), SUB) for t in range(tiles)]
            q = jnp.concatenate([qp[x, cols] for x in spans], axis=0)
            m, pn, pd = attend(jnp.where(mine, q, jnp.zeros_like(q)), k, v)
            for t, x in enumerate(spans):
                y = slice(t * SUB, (t + 1) * SUB)
                merge(x, cols, mine, m[y], pn[y], pd[y])
            res = pn / pd
            kept = res if s == 0 else jnp.where(first, kept, res)
        far_ref[:, cols] = kept.astype(jnp.bfloat16)

    def take_near(cut):
        near_copy(cut, 0).wait_recv()
        near_copy(cut, 1).wait_recv()

    early = [(d, cut) for d in range(1, rounds + 1) for cut in range(CUTS)]
    share = -(-len(early) // PAIRS) if early else 0
    half = (rounds + 1) // 2
    low, high = range(1, half + 1), range(half + 1, rounds + 1)

    def phase_one(p, _):
        @pl.when(p == PAIRS - 3)
        def _():
            take_near(0)
            select(1, 0, pk, pv)

        near(p, k_ref, v_ref, True)
        for x in range(PAIRS):
            todo = early[x * share:(x + 1) * share]

            @pl.when(p == x)
            def _():
                for d, cut in todo:
                    relay(0, d, cut)

        @pl.when(p == PAIRS - 3)
        def _():
            send(1, 0)
        return 0

    lax.fori_loop(0, PAIRS, phase_one, 0)
    if n > group:
        for i in range(n - group):
            far_copy(i).start()
    gets = {0: 1, 3: 2, 6: 3}
    passes = {0: (low, 0), 1: (high, 0), 2: (low, 1), 3: (high, 1), 4: (low, 2), 5: (high, 2)}

    def phase_two(p, _):
        for x, cut in gets.items():
            @pl.when(p == x)
            def _():
                take_near(cut)
                select(1, cut, pk, pv)

        for x in range(CUTS):
            @pl.when(p == x * PER_CUT)
            def _():
                if length > 1 and x < CUTS - 1:
                    arrive(0, length - 1, x)

        near(p, pk, pv, False)
        middle(p, 0)
        for x in range(PAIRS):
            @pl.when(p == x)
            def _():
                if x in passes:
                    for d in passes[x][0]:
                        relay(1, d, passes[x][1])
                if x in gets and gets[x] < CUTS - 1:
                    send(1, gets[x])
        return 0

    split = PAIRS - PER_CUT
    lax.fori_loop(0, split, phase_two, 0)
    if length > 1:
        arrive(0, length - 1, CUTS - 1)
        cross(length - 1, lambda c: c.start())
    if n > group:
        for i in range(n - group):
            far_copy(i, True).wait_recv()

    def phase_three(p, _):
        for x in range(CUTS):
            @pl.when(p == x * PER_CUT)
            def _():
                for d in range(1 if x == CUTS - 1 else max(1, length - 1), length):
                    arrive(1, d, x)

        middle(p, 1)
        far(p)
        cols = lanes_of(p)
        for t in range(tiles):
            span = slice(t * TILE, (t + 1) * TILE)
            res = (num[span, cols] / den[span, cols]).astype(jnp.bfloat16)
            out_ref[span, cols] = jnp.dot(back[...], res, preferred_element_type=jnp.float32).astype(jnp.bfloat16)
        return 0

    early_split = split - PER_CUT
    lax.fori_loop(0, early_split, phase_three, 0)
    lax.fori_loop(split, PAIRS, phase_two, 0)
    lax.fori_loop(early_split, PAIRS, phase_three, 0)
    for cut in range(CUTS):
        for which in range(2):
            near_copy(cut, which).wait_send()
        for u in range(2 if cut < CUTS - 1 else 1):
            for d in range(max(1, length - 1)):
                both(u, d, cut, lambda c: c.wait_send())
    for d in range(1, length):
        cross(d, lambda c: c.wait_send())
    for i in range(n - group):
        far_copy(i).wait_send()


def per_device(queries, keys, values):
    n = lax.axis_size("seq")
    group = min(GROUP, n)
    length = group // 2
    rows, cols = queries.shape
    spare = n - group
    dma = pltpu.SemaphoreType.DMA
    vmem = pl.BlockSpec(memory_space=pltpu.VMEM)
    return pl.pallas_call(
        functools.partial(kernel, n, group),
        out_shape=(
            jax.ShapeDtypeStruct((rows, cols), jnp.bfloat16),
            jax.ShapeDtypeStruct((rows // FAR, cols), jnp.bfloat16),
        ),
        in_specs=[vmem] * 3,
        out_specs=(vmem, vmem),
        scratch_shapes=[
            pltpu.VMEM((rows, cols), jnp.bfloat16),
            pltpu.VMEM((rows, cols), jnp.bfloat16),
            pltpu.VMEM((group, CUTS, rows // MID, 2 * CUT), jnp.bfloat16),
            pltpu.VMEM((spare + 1, CUTS, rows // FAR, 2 * CUT), jnp.bfloat16),
            pltpu.VMEM((rows, cols), jnp.bfloat16),
            pltpu.VMEM((rows, cols), jnp.float32),
            pltpu.VMEM((rows, cols), jnp.float32),
            pltpu.VMEM((rows, cols), jnp.float32),
            pltpu.VMEM((TILE, TILE), jnp.bfloat16),
            pltpu.VMEM((TILE, TILE), jnp.bfloat16),
            dma((2, CUTS)),
            dma((2, CUTS)),
            dma((2, 2, length, CUTS)),
            dma((group, CUTS)),
            dma((spare + 1,)),
            dma((spare + 1,)),
            dma((2, length)),
        ],
        compiler_params=pltpu.CompilerParams(collective_id=0, has_side_effects=True, vmem_limit_bytes=62 << 20),
    )(queries, keys, values)


def solution(mesh):
    spec = P(("dp", "seq"), None)
    return jax.shard_map(per_device, mesh=mesh, in_specs=(spec, spec, spec), out_specs=(spec, spec), check_vma=False)
```
